32 devices in a mesh: dp: 8 (over y, x, core), tensor: 4 (over z).
Axes of the slice: x: 2, y: 2, z: 4, core: 2. Of those that a mesh axis runs over, the one named last changes fastest.
Arguments:
- x_in: bfloat16 [2048, 768], P(('dp', 'tensor')), may hold values from -6 to 6
- segment_ids: int32 [2048], P('dp'), may hold values from 0 to 2, as said below
- norm_gain: float32 [2, 768], replicated, may hold values from 0.1 to 1.9
- w_zx: bfloat16 [2, 768, 2, 1536], P(None, 'dp', None, 'tensor'), may hold values from -0.21875 to 0.21875
- w_dt: bfloat16 [2, 768, 24], P(None, 'dp', 'tensor'), may hold values from -0.21875 to 0.21875
- w_bc: bfloat16 [2, 768, 256], P(None, 'dp'), may hold values from -0.21875 to 0.21875
- conv_x: float32 [2, 4, 1536], P(None, None, 'tensor'), may hold values from -3 to 3
- conv_x_bias: float32 [2, 1536], P(None, 'tensor'), may hold values from -2 to 2
- conv_bc: float32 [2, 4, 256], replicated, may hold values from -3 to 3
- conv_bc_bias: float32 [2, 256], replicated, may hold values from -2 to 2
- dt_bias: float32 [2, 24], P(None, 'tensor'), may hold values from -7 to -2
- a_log: float32 [2, 24], P(None, 'tensor'), may hold values from 0 to 1.5
- d_skip: float32 [2, 24], P(None, 'tensor'), may hold values from 0.5 to 1.5
- gate_gain: float32 [2, 1536], P(None, 'tensor'), may hold values from 0.1 to 1.9
- w_out: bfloat16 [2, 1536, 768], P(None, 'tensor', 'dp'), may hold values from -0.15625 to 0.15625
- cotangent: bfloat16 [2048, 768], P(('dp', 'tensor')), may hold values from -6 to 6
Outputs:
- y_out: bfloat16 [2048, 768], P(('dp', 'tensor'))
- d_x_in: float32 [2048, 768], P(('dp', 'tensor'))
- d_norm_gain: float32 [2, 768], replicated
- d_w_zx: float32 [2, 768, 2, 1536], P(None, 'dp', None, 'tensor')
- d_w_dt: float32 [2, 768, 24], P(None, 'dp', 'tensor')
- d_w_bc: float32 [2, 768, 256], P(None, 'dp')
- d_conv_x: float32 [2, 4, 1536], replicated
- d_conv_x_bias: float32 [2, 1536], replicated
- d_conv_bc: float32 [2, 4, 256], replicated
- d_conv_bc_bias: float32 [2, 256], replicated
- d_dt_bias: float32 [2, 24], replicated
- d_a_log: float32 [2, 24], replicated
- d_d_skip: float32 [2, 24], replicated
- d_gate_gain: float32 [2, 1536], replicated
- d_w_out: float32 [2, 1536, 768], P(None, 'tensor', 'dp')
The draws below stay inside these ranges and needn't reach their ends.
Inputs may be any that keep to these rules, and one draw needn't show every extreme that they name: `segment_ids`: segment numbers start at 0 and rise by one at each new sequence; every sequence but the first and the last has exactly 1024 tokens, the first has 1 to 1023 tokens.
All inputs are finite; a program needn't handle non-finite values.
Results may differ from the reference program's by a relative error of at most 0.012.
The reference program's roundings to bfloat16 on the way count: a program that leaves them out, or rounds other values in their place, can miss the bound.
Values may be sent and summed in bfloat16 or wider, within the bound.
A program may use at most 128 MiB of HBM per device.

```python
import jax
import jax.numpy as jnp
from jax import lax

D = 768
HEADS = 24
HEAD_DIM = 64
STATE = 128
CONV = 4
STRETCH = 256
LAYERS = 2
SEQ_LEN = 1024
INNER = 1536
TOKENS = 2048


def draw_segment_ids(key, part):
    offset = jax.random.randint(key, (), 1, SEQ_LEN)
    places = jnp.arange(TOKENS, dtype=jnp.int32)
    return ((places + offset) // SEQ_LEN).astype(jnp.int32)


def level_of(rng, extent, cuts, smallest, largest):
    def one(position, shards_of):
        steps = jax.random.uniform(jax.random.fold_in(jax.random.fold_in(rng, 6), position), (shards_of,), jnp.float32, smallest / len(cuts), largest / len(cuts))
        return jnp.repeat(jnp.exp(steps), extent[position] // shards_of).reshape((-1,) + (1,) * (len(extent) - position - 1))

    level = one(*cuts[0])
    for cut in cuts[1:]:
        level = level * one(*cut)
    return level


def scatter_about(rng, dims, spread, bound, shards=(), kind=jnp.bfloat16):
    entries = jax.random.normal(rng, dims, jnp.float32) * spread
    if len(shards) > 0:
        entries = level_of(rng, dims, shards, -0.22, 0.18) * entries
    return jnp.clip(entries, min=-bound, max=bound).astype(kind)


def setup_inputs(seed: int = 0) -> dict:
    key_list = jax.random.split(jax.random.key(seed), 17)
    x_in = scatter_about(key_list[0], (TOKENS, D), 1.0, 6.0, ((0, 32),))
    segment_ids = draw_segment_ids(jax.random.fold_in(key_list[16], 71), 0)
    norm_gain = jnp.clip(1.0 + 0.18 * jax.random.normal(key_list[2], (LAYERS, D), jnp.float32), 0.1, 1.9)
    w_zx = scatter_about(key_list[3], (LAYERS, D, 2, INNER), D ** -0.5, 0.21875, ((1, 8), (3, 4)))
    w_dt = scatter_about(key_list[4], (LAYERS, D, HEADS), D ** -0.5, 0.21875, ((1, 8), (2, 4)))
    w_bc = scatter_about(key_list[5], (LAYERS, D, 2 * STATE), D ** -0.5, 0.21875, ((1, 8),))
    conv_x = scatter_about(key_list[6], (LAYERS, CONV, INNER), 0.5, 3.0, ((2, 4),), jnp.float32)
    conv_x_bias = scatter_about(key_list[7], (LAYERS, INNER), 0.3, 2.0, ((1, 4),), jnp.float32)
    conv_bc = scatter_about(key_list[8], (LAYERS, CONV, 2 * STATE), 0.5, 3.0, (), jnp.float32)
    conv_bc_bias = scatter_about(key_list[9], (LAYERS, 2 * STATE), 0.3, 2.0, (), jnp.float32)
    dt_bias = jnp.clip(-7.0 + 5.0 * jax.random.uniform(key_list[10], (LAYERS, HEADS), jnp.float32) ** level_of(key_list[10], (LAYERS, HEADS), ((1, 4),), -0.2, 0.2), -7.0, -2.0)
    a_log = jnp.clip(1.5 * jax.random.uniform(key_list[11], (LAYERS, HEADS), jnp.float32) ** level_of(key_list[11], (LAYERS, HEADS), ((1, 4),), -0.2, 0.2), 0.0, 1.5)
    d_skip = jnp.clip(0.5 + 1.0 * jax.random.uniform(key_list[12], (LAYERS, HEADS), jnp.float32) ** level_of(key_list[12], (LAYERS, HEADS), ((1, 4),), -0.2, 0.2), 0.5, 1.5)
    gate_gain = jnp.clip(1.0 + 0.18 * jax.random.normal(key_list[13], (LAYERS, INNER), jnp.float32), 0.1, 1.9)
    w_out = scatter_about(key_list[14], (LAYERS, INNER, D), INNER ** -0.5, 0.15625, ((1, 4), (2, 8)))
    cotangent = scatter_about(key_list[15], (TOKENS, D), 1.0, 6.0, ((0, 32),))
    return dict(x_in=x_in, segment_ids=segment_ids, norm_gain=norm_gain, w_zx=w_zx, w_dt=w_dt, w_bc=w_bc, conv_x=conv_x, conv_x_bias=conv_x_bias, conv_bc=conv_bc, conv_bc_bias=conv_bc_bias, dt_bias=dt_bias, a_log=a_log, d_skip=d_skip, gate_gain=gate_gain, w_out=w_out, cotangent=cotangent)


EPSILON = 1e-05
PRECISE = lax.Precision.HIGHEST

@jax.custom_vjp
def low(v):
    return lax.optimization_barrier(v.astype(jnp.bfloat16)).astype(jnp.float32)

@jax.custom_vjp
def low_back(v):
    return v

def low_keep(v):
    return (low(v), None)

def low_pass(kept, grad):
    return (grad,)

def back_keep(v):
    return (v, None)

def back_low(kept, grad):
    return (low(grad),)
low.defvjp(low_keep, low_pass)
low_back.defvjp(back_keep, back_low)

def stretch_core(xs_block, b_block, c_block, dt_block, la_block, skip_gain, seg_block, seg_before, state_in):
    cumulative = jnp.cumsum(la_block, axis=0)
    length = seg_block.shape[0]
    places = jnp.arange(length)
    inside = (seg_block[:, None] == seg_block[None, :]) & (places[:, None] >= places[None, :])
    span_logs = cumulative[:, None, :] - cumulative[None, :, :]
    decays = jnp.exp(jnp.where(inside[:, :, None], span_logs, -1e+30))
    scores = jnp.dot(c_block, b_block.T, precision=PRECISE)
    scaled = xs_block * dt_block[:, :, None]
    output = jnp.einsum('ijh,ij,jhp->ihp', decays, scores, scaled, precision=PRECISE)
    reached = (seg_block == seg_before).astype(jnp.float32)
    carried = jnp.einsum('in,hpn->ihp', c_block, state_in, precision=PRECISE)
    output = output + jnp.exp(cumulative)[:, :, None] * reached[:, None, None] * carried
    output = output + skip_gain[None, :, None] * xs_block
    last_seg = seg_block[length - 1]
    kept_rows = (seg_block == last_seg).astype(jnp.float32)
    to_end = jnp.exp(cumulative[length - 1][None, :] - cumulative) * kept_rows[:, None]
    whole_seg = (last_seg == seg_before).astype(jnp.float32)
    new_state = (whole_seg * jnp.exp(cumulative[length - 1]))[:, None, None] * state_in
    new_state = new_state + jnp.einsum('jh,jhp,jn->hpn', to_end, scaled, b_block, precision=PRECISE)
    return (output, new_state)

def conv_apply(extended, seg_extended, segments, conv_weight, conv_bias):
    length = segments.shape[0]
    tap_count = conv_weight.shape[0]
    result = jnp.zeros((length, extended.shape[1]), jnp.float32) + conv_bias
    for tap_index in range(tap_count):
        same_seg = (seg_extended[tap_index:tap_index + length] == segments).astype(jnp.float32)
        result = result + conv_weight[tap_index] * extended[tap_index:tap_index + length] * same_seg[:, None]
    return result

def run_layer(hidden, seg_blocks, seg_windows, seg_before, params):
    gain, w_zpart, w_xpart, w_dtpart, w_bcpart, conv_weight, conv_bias, bias_dt, log_rate, skip_gain, gate_weight, w_outpart = params
    margin = CONV - 1

    def advance(carry, pieces):
        tail_rows, state_in = carry
        rows_in, seg_block, seg_window, before_seg = pieces
        rms_scale = lax.rsqrt(lax.optimization_barrier(jnp.mean(rows_in * rows_in, axis=1, keepdims=True)) + EPSILON)
        normed = low(rows_in * rms_scale * gain)
        proj_z = low_back(jnp.dot(normed, w_zpart, precision=PRECISE))
        proj_x = low(low_back(jnp.dot(normed, w_xpart, precision=PRECISE)))
        proj_dt = low_back(jnp.dot(normed, w_dtpart, precision=PRECISE))
        proj_bc = low(jnp.dot(normed, w_bcpart, precision=PRECISE))
        conv_in = jnp.concatenate([proj_x, proj_bc], axis=1)
        extended = jnp.concatenate([tail_rows, conv_in], axis=0)
        activated = jax.nn.silu(conv_apply(extended, seg_window, seg_block, conv_weight, conv_bias))
        xs_heads = activated[:, :INNER].reshape(STRETCH, HEADS, HEAD_DIM)
        b_mat = activated[:, INNER:INNER + STATE]
        c_mat = activated[:, INNER + STATE:]
        step_dt = jax.nn.softplus(proj_dt + bias_dt)
        log_decay = -step_dt * jnp.exp(log_rate)
        heads_y, state_out = stretch_core(xs_heads, b_mat, c_mat, step_dt, log_decay, skip_gain, seg_block, before_seg, state_in)
        gated_y = heads_y.reshape(STRETCH, INNER) * jax.nn.silu(proj_z)
        mixed_out = low(gated_y * lax.rsqrt(lax.optimization_barrier(jnp.mean(gated_y * gated_y, axis=1, keepdims=True)) + EPSILON) * gate_weight)
        branch = low_back(jnp.dot(mixed_out, w_outpart, precision=PRECISE))
        return ((extended[STRETCH:], state_out), rows_in + branch)
    start_carry = (jnp.zeros((margin, INNER + 2 * STATE), jnp.float32), jnp.zeros((HEADS, HEAD_DIM, STATE), jnp.float32))
    block_count = hidden.shape[0] // STRETCH
    finals, outputs = lax.scan(jax.checkpoint(advance), start_carry, (hidden.reshape(block_count, STRETCH, D), seg_blocks, seg_windows, seg_before))
    return outputs.reshape(hidden.shape[0], D)

def reference(x_in, segment_ids, norm_gain, w_zx, w_dt, w_bc, conv_x, conv_x_bias, conv_bc, conv_bc_bias, dt_bias, a_log, d_skip, gate_gain, w_out, cotangent):
    token_count = x_in.shape[0]
    block_count = token_count // STRETCH
    margin = CONV - 1
    padded = jnp.concatenate([jnp.full((margin,), -1, jnp.int32), segment_ids.astype(jnp.int32)])
    window_index = (jnp.arange(block_count, dtype=jnp.int32)[:, None] * STRETCH + jnp.arange(STRETCH + margin, dtype=jnp.int32)[None, :]).astype(jnp.int32)
    seg_windows = padded[window_index]
    seg_blocks = segment_ids.astype(jnp.int32).reshape(block_count, STRETCH)
    seg_before = seg_windows[:, margin - 1]

    def forward(hidden, gain_all, zx_all, dt_all, bc_all, convx_all, convxb_all, convbc_all, convbcb_all, dtb_all, alog_all, skip_all, gate_all, out_all):
        for layer_num in range(LAYERS):
            params = (gain_all[layer_num], zx_all[layer_num][:, 0, :], zx_all[layer_num][:, 1, :], dt_all[layer_num], bc_all[layer_num], jnp.concatenate([convx_all[layer_num], convbc_all[layer_num]], axis=1), jnp.concatenate([convxb_all[layer_num], convbcb_all[layer_num]]), dtb_all[layer_num], alog_all[layer_num], skip_all[layer_num], gate_all[layer_num], out_all[layer_num])
            hidden = run_layer(hidden, seg_blocks, seg_windows, seg_before, params)
        return hidden
    result, pullback = jax.vjp(forward, x_in.astype(jnp.float32), norm_gain.astype(jnp.float32), w_zx.astype(jnp.float32), w_dt.astype(jnp.float32), w_bc.astype(jnp.float32), conv_x.astype(jnp.float32), conv_x_bias.astype(jnp.float32), conv_bc.astype(jnp.float32), conv_bc_bias.astype(jnp.float32), dt_bias.astype(jnp.float32), a_log.astype(jnp.float32), d_skip.astype(jnp.float32), gate_gain.astype(jnp.float32), w_out.astype(jnp.float32))
    grads = pullback(cotangent.astype(jnp.float32))
    return (result.astype(jnp.bfloat16), grads[0], grads[1], grads[2], grads[3], grads[4], grads[5], grads[6], grads[7], grads[8], grads[9], grads[10], grads[11], grads[12], grads[13])
```

```python
import jax
import jax.numpy as jnp
from jax import lax
from jax.experimental import pallas as pl
from jax.experimental.pallas import tpu as pltpu
from jax.sharding import PartitionSpec as P

EPSILON = 1e-05
PRECISE = lax.Precision.HIGHEST
CORE = lax.Precision.HIGH
MESH = pl.DeviceIdType.MESH


def exchange(parts, axis, collective_id):
    count = lax.axis_size(axis)
    many = len(parts)
    block_shapes = [a.shape[1:] if scatter else a.shape for a, scatter, _ in parts]
    outs, slots = [], []
    for (a, _, reduce), shape in zip(parts, block_shapes):
        if reduce:
            outs.append(jax.ShapeDtypeStruct(shape, jnp.float32))
            slots.append(pltpu.VMEM((count,) + shape, a.dtype))
        else:
            outs.append(jax.ShapeDtypeStruct((count,) + shape, a.dtype))

    def kernel(*refs):
        ins, results = refs[:many], refs[many : 2 * many]
        scratch = list(refs[2 * many : len(refs) - 3])
        send_sem, recv_sem, own_sem = refs[len(refs) - 3 :]
        landing = [
            scratch.pop(0) if reduce else results[i] for i, (_, _, reduce) in enumerate(parts)
        ]
        me = lax.axis_index(axis)
        barrier = pltpu.get_barrier_semaphore()
        for step in range(1, count):
            peer = lax.rem(me + step, count)
            pl.semaphore_signal(barrier, inc=1, device_id={axis: peer}, device_id_type=MESH)
        own = []
        for i, (_, scatter, _) in enumerate(parts):
            block = ins[i].at[me] if scatter else ins[i]
            copy = pltpu.make_async_copy(block, landing[i].at[me], own_sem.at[i])
            copy.start()
            own.append(copy)
        pl.semaphore_wait(barrier, count - 1)
        sent = []
        for step in range(1, count):
            peer = lax.rem(me + step, count)
            for i, (_, scatter, _) in enumerate(parts):
                copy = pltpu.make_async_remote_copy(
                    src_ref=ins[i].at[peer] if scatter else ins[i],
                    dst_ref=landing[i].at[me],
                    send_sem=send_sem.at[i, step - 1],
                    recv_sem=recv_sem.at[i, step - 1],
                    device_id={axis: peer},
                    device_id_type=MESH,
                )
                copy.start()
                sent.append(copy)
        for copy in own:
            copy.wait()
        for copy in sent:
            copy.wait()
        for i, (_, _, reduce) in enumerate(parts):
            if reduce:
                total = landing[i][0].astype(jnp.float32)
                for source in range(1, count):
                    total = total + landing[i][source].astype(jnp.float32)
                results[i][...] = total

    return pl.pallas_call(
        kernel,
        out_shape=tuple(outs),
        in_specs=[pl.BlockSpec(memory_space=pltpu.VMEM)] * many,
        out_specs=tuple([pl.BlockSpec(memory_space=pltpu.VMEM)] * many),
        scratch_shapes=slots
        + [
            pltpu.SemaphoreType.DMA((many, count - 1)),
            pltpu.SemaphoreType.DMA((many, count - 1)),
            pltpu.SemaphoreType.DMA((many,)),
        ],
        compiler_params=pltpu.CompilerParams(collective_id=collective_id, has_side_effects=True),
    )(*[a for a, _, _ in parts])


def rows_from_all(rows, collective_id):
    (out,) = exchange([(rows, False, False)], "tensor", collective_id)
    return out.reshape(-1, rows.shape[1])


def rows_summed(partial_rows, collective_id):
    count = lax.axis_size("tensor")
    blocks = partial_rows.astype(jnp.bfloat16).reshape(count, -1, partial_rows.shape[1])
    return exchange([(blocks, True, True)], "tensor", collective_id)[0]


def token_sums(values, collective_id):
    length = values.shape[0]
    return exchange([(values.reshape(-1, 128), False, True)], "tensor", collective_id)[0].reshape(
        length
    )


def passed_along(block, axis, distance):
    devices = range(lax.axis_size(axis))
    route = [(i - distance, i) for i in devices if i - distance in devices]
    return lax.ppermute(block, axis, route)


def entering(coefficients, values, backward):
    count = values.shape[0]
    place = lax.axis_index("dp")
    state = jnp.zeros(values.shape[1:], jnp.float32)
    for source in reversed(range(count)) if backward else range(count):
        ahead = source > place if backward else source < place
        later = values[source].astype(jnp.float32) + coefficients[source][:, None, None] * state
        state = jnp.where(ahead, later, state)
    return state


def mixer_core(xs_heads, b_mat, c_mat, step_dt, log_decay, skip_gain, segments):
    length = segments.shape[0]
    places = jnp.arange(length)
    below = places[:, None] >= places[None, :]
    cumulative = jnp.dot(below.astype(jnp.float32), log_decay, precision=PRECISE)
    inside = (segments[:, None] == segments[None, :]) & below
    by_head = cumulative.T
    span_logs = by_head[:, :, None] - by_head[:, None, :]
    decays = jnp.exp(jnp.where(inside[None], span_logs, -1e30))
    scores = jnp.dot(c_mat, b_mat.T, precision=CORE)
    scaled = xs_heads * step_dt[:, :, None]
    output = jnp.einsum("hij,jhp->ihp", decays * scores[None], scaled, precision=CORE)
    output = output + skip_gain[None, :, None] * xs_heads
    kept_rows = (segments == segments[length - 1]).astype(jnp.float32)
    to_end = jnp.exp(cumulative[length - 1][None, :] - cumulative) * kept_rows[:, None]
    state = jnp.einsum("jhp,jn->hpn", scaled * to_end[:, :, None], b_mat, precision=CORE)
    return (output, state, cumulative)


def init_output(cumulative, c_mat, start_state, segments):
    reached = (segments == segments[0]).astype(jnp.float32)
    carried = jnp.einsum("tn,hpn->thp", c_mat, start_state, precision=CORE)
    return (jnp.exp(cumulative) * reached[:, None])[:, :, None] * carried


def conv_apply(extended, seg_extended, segments, conv_weight, conv_bias):
    length = segments.shape[0]
    tap_count = conv_weight.shape[0]
    result = jnp.zeros((length, extended.shape[1]), jnp.float32) + conv_bias
    for tap_index in range(tap_count):
        same_seg = (seg_extended[tap_index : tap_index + length] == segments).astype(jnp.float32)
        result = (
            result
            + conv_weight[tap_index] * extended[tap_index : tap_index + length] * same_seg[:, None]
        )
    return result


def mixer_front(
    extended,
    proj_dt,
    conv_weight,
    conv_bias,
    bias_dt,
    log_rate,
    seg_extended,
    segments,
    head_count,
    inner_width,
):
    activated = jax.nn.silu(conv_apply(extended, seg_extended, segments, conv_weight, conv_bias))
    length = segments.shape[0]
    state_width = (activated.shape[1] - inner_width) // 2
    xs_heads = activated[:, :inner_width].reshape(length, head_count, inner_width // head_count)
    b_mat = activated[:, inner_width : inner_width + state_width]
    c_mat = activated[:, inner_width + state_width :]
    step_dt = jax.nn.softplus(proj_dt + bias_dt)
    log_decay = -step_dt * jnp.exp(log_rate)
    return (xs_heads, b_mat, c_mat, step_dt, log_decay)


def local(
    x_in,
    segment_ids,
    norm_gain,
    w_zx,
    w_dt,
    w_bc,
    conv_x,
    conv_x_bias,
    conv_bc,
    conv_bc_bias,
    dt_bias,
    a_log,
    d_skip,
    gate_gain,
    w_out,
    cotangent,
):
    layers = norm_gain.shape[0]
    tensor_count = lax.axis_size("tensor")
    data_count = lax.axis_size("dp")
    model_width = x_in.shape[1]
    shard_rows = segment_ids.shape[0]
    local_inner = conv_x.shape[2]
    local_heads = dt_bias.shape[1]
    state_pair = w_bc.shape[2]
    state_width = state_pair // 2
    head_width = local_inner // local_heads
    full_inner = local_inner * tensor_count
    margin = conv_x.shape[1] - 1
    dt_room = -local_heads % 128 + local_heads
    at_bc = 2 * local_inner
    at_dt = at_bc + state_pair
    at_out = at_dt + dt_room
    width = at_out + local_inner
    ids = iter(range(1, 64))

    packed = [
        jnp.concatenate(
            [
                w_zx[l].reshape(-1, at_bc),
                w_bc[l],
                jnp.pad(w_dt[l], ((0, 0), (0, dt_room - local_heads))),
                w_out[l].T,
            ],
            axis=1,
        )
        for l in range(layers)
    ]
    weights_all = []
    for l in range(layers):
        if l == 0:
            (full,) = exchange([(packed[l], False, False)], "dp", next(ids))
            weights_all.append(full.reshape(model_width, width))
        else:
            weights_all.append(lax.all_gather(packed[l], "dp", axis=0, tiled=True))

    seg_tail = (segment_ids[shard_rows - margin :] + 1).astype(jnp.bfloat16)
    tail_segs = passed_along(seg_tail, "dp", 1)
    seg_extended = jnp.concatenate([tail_segs.astype(jnp.int32) - 1, segment_ids])
    joined = (seg_extended[margin - 1] == segment_ids[0]).astype(jnp.float32)
    whole_seg = (segment_ids[shard_rows - 1] == segment_ids[0]).astype(jnp.float32)

    hidden = x_in.astype(jnp.float32)
    records = []
    for layer_num in range(layers):
        weights = weights_all[layer_num]
        rms_scale = lax.rsqrt(jnp.mean(hidden * hidden, axis=1, keepdims=True) + EPSILON)
        normed = (hidden * rms_scale * norm_gain[layer_num]).astype(jnp.bfloat16)
        gathered = rows_from_all(normed, next(ids))
        projected = jnp.dot(gathered, weights[:, :at_out], preferred_element_type=jnp.float32)
        proj_z = projected[:, :local_inner]
        proj_dt = projected[:, at_dt : at_dt + local_heads]
        conv_in = projected[:, local_inner:at_dt].astype(jnp.bfloat16)
        tail_rows = passed_along(conv_in[shard_rows - margin :], "dp", 1)
        extended = jnp.concatenate([tail_rows, conv_in], axis=0).astype(jnp.float32)
        conv_weight = jnp.concatenate([conv_x[layer_num], conv_bc[layer_num]], axis=1)
        conv_bias = jnp.concatenate([conv_x_bias[layer_num], conv_bc_bias[layer_num]])

        def front_fn(extended, proj_dt, conv_weight, conv_bias, bias_dt, log_rate):
            return mixer_front(
                extended,
                proj_dt,
                conv_weight,
                conv_bias,
                bias_dt,
                log_rate,
                seg_extended,
                segment_ids,
                local_heads,
                local_inner,
            )

        front_vals, front_back = jax.vjp(
            front_fn,
            extended,
            proj_dt,
            conv_weight,
            conv_bias,
            dt_bias[layer_num],
            a_log[layer_num],
        )
        xs_heads, b_mat, c_mat, step_dt, log_decay = front_vals
        core_vals, core_back = jax.vjp(
            lambda *args: mixer_core(*args, segment_ids),
            xs_heads,
            b_mat,
            c_mat,
            step_dt,
            log_decay,
            d_skip[layer_num],
        )
        local_y, local_state, cumulative = core_vals
        end_decay = jnp.exp(cumulative[shard_rows - 1])
        coefficient = joined * whole_seg * end_decay
        coefficients, states = exchange(
            [
                (jnp.pad(coefficient, (0, dt_room - local_heads)).reshape(-1, 128), False, False),
                (
                    local_state.astype(jnp.bfloat16).reshape(local_inner, state_width),
                    False,
                    False,
                ),
            ],
            "dp",
            next(ids),
        )
        coefficients = coefficients.reshape(data_count, dt_room)[:, :local_heads]
        states = states.reshape(data_count, local_heads, head_width, state_width)
        start_state = joined * entering(coefficients, states, False)
        init_y, init_back = jax.vjp(
            lambda *args: init_output(*args, segment_ids), cumulative, c_mat, start_state
        )
        ssd_y = (local_y + init_y).reshape(shard_rows, local_inner)
        gate_vals = jax.nn.silu(proj_z)
        gated_y = ssd_y * gate_vals
        squares = token_sums(jnp.sum(gated_y * gated_y, axis=1), next(ids))
        inverse = lax.rsqrt(squares / full_inner + EPSILON)
        mixed_out = (gated_y * inverse[:, None] * gate_gain[layer_num]).astype(jnp.bfloat16)
        branch = rows_summed(
            jnp.einsum(
                "tk,dk->td",
                mixed_out,
                weights[:, at_out:],
                preferred_element_type=jnp.float32,
            ),
            next(ids),
        )
        records.append(
            (
                hidden,
                gathered,
                proj_z,
                ssd_y,
                gate_vals,
                gated_y,
                mixed_out,
                inverse,
                start_state,
                end_decay,
                coefficients,
                front_back,
                core_back,
                init_back,
            )
        )
        hidden = hidden + branch
    y_out = hidden.astype(jnp.bfloat16)
    grad_hidden = cotangent.astype(jnp.float32)
    weight_grads = [None] * layers
    small_grads = [None] * layers
    for layer_num in reversed(range(layers)):
        (
            hidden_in,
            gathered,
            proj_z,
            ssd_y,
            gate_vals,
            gated_y,
            mixed_out,
            inverse,
            start_state,
            end_decay,
            coefficients,
            front_back,
            core_back,
            init_back,
        ) = records[layer_num]
        weights = weights_all[layer_num]
        branch_grad = rows_from_all(grad_hidden.astype(jnp.bfloat16), next(ids))
        d_out = jnp.einsum("td,tk->dk", branch_grad, mixed_out, preferred_element_type=jnp.float32)
        d_mixed = jnp.einsum(
            "td,dk->tk", branch_grad, weights[:, at_out:], preferred_element_type=jnp.float32
        )
        weighted = d_mixed * gate_gain[layer_num]
        inner_dot = token_sums(jnp.sum(weighted * gated_y, axis=1), next(ids))
        d_gated = (
            inverse[:, None] * weighted
            - gated_y * (inverse * inverse * inverse * inner_dot / full_inner)[:, None]
        )
        d_gate_gain = jnp.sum(d_mixed * gated_y * inverse[:, None], axis=0)
        d_ssd = d_gated * gate_vals
        sigmoid_z = jax.nn.sigmoid(proj_z)
        d_proj_z = (d_gated * ssd_y * sigmoid_z * (1.0 + proj_z * (1.0 - sigmoid_z))).astype(
            jnp.bfloat16
        )
        d_heads = d_ssd.reshape(shard_rows, local_heads, head_width)
        d_cum, d_cmat_first, d_start = init_back(d_heads)
        (d_states,) = exchange(
            [
                (
                    (joined * d_start).astype(jnp.bfloat16).reshape(local_inner, state_width),
                    False,
                    False,
                )
            ],
            "dp",
            next(ids),
        )
        d_end = entering(
            coefficients,
            d_states.reshape(data_count, local_heads, head_width, state_width),
            True,
        )
        d_last = whole_seg * end_decay * jnp.sum(d_end * start_state, axis=(1, 2))
        d_cum = d_cum + jnp.where(
            jnp.arange(shard_rows)[:, None] == shard_rows - 1, d_last[None, :], 0.0
        )
        d_xs, d_bmat, d_cmat_second, d_dt, d_decay, d_skip_grad = core_back((d_heads, d_end, d_cum))
        d_ext, d_proj_dt, d_conv_w, d_conv_b, d_dt_bias, d_log_rate = front_back(
            (d_xs, d_bmat, d_cmat_first + d_cmat_second, d_dt, d_decay)
        )
        from_next = passed_along(d_ext[:margin], "dp", -1)
        d_conv_in = d_ext[margin:]
        d_conv_in = jnp.concatenate(
            [d_conv_in[: shard_rows - margin], d_conv_in[shard_rows - margin :] + from_next], axis=0
        )
        d_proj_bc = d_conv_in[:, local_inner:]
        bc_high = d_proj_bc.astype(jnp.bfloat16)
        bc_rest = (d_proj_bc - bc_high.astype(jnp.float32)).astype(jnp.bfloat16)
        d_all = jnp.concatenate(
            [
                d_proj_z,
                d_conv_in[:, :local_inner].astype(jnp.bfloat16),
                bc_high,
                jnp.pad(
                    d_proj_dt.astype(jnp.bfloat16), ((0, 0), (0, dt_room - local_heads))
                ),
            ],
            axis=1,
        )
        d_normed = rows_summed(
            jnp.einsum(
                "tk,dk->td", d_all, weights[:, :at_out], preferred_element_type=jnp.float32
            )
            + jnp.einsum(
                "tk,dk->td", bc_rest, weights[:, at_bc:at_dt], preferred_element_type=jnp.float32
            ),
            next(ids),
        )
        d_in = jnp.einsum("td,tk->dk", gathered, d_all, preferred_element_type=jnp.float32)
        d_rest = jnp.einsum("td,tk->dk", gathered, bc_rest, preferred_element_type=jnp.float32)
        weight_grads[layer_num] = jnp.concatenate(
            [
                d_in[:, :at_bc].astype(jnp.bfloat16),
                (d_in[:, at_bc:at_dt] + d_rest).astype(jnp.bfloat16),
                d_in[:, at_dt:].astype(jnp.bfloat16),
                d_out.astype(jnp.bfloat16),
            ],
            axis=1,
        ).reshape(data_count, model_width // data_count, width)
        rms_scale = lax.rsqrt(jnp.mean(hidden_in * hidden_in, axis=1, keepdims=True) + EPSILON)
        gain_grad_in = d_normed * norm_gain[layer_num]
        d_norm_gain = jnp.sum(d_normed * hidden_in * rms_scale, axis=0)
        grad_hidden = (
            grad_hidden
            + rms_scale * gain_grad_in
            - hidden_in
            * rms_scale
            * rms_scale
            * rms_scale
            * jnp.mean(gain_grad_in * hidden_in, axis=1, keepdims=True)
        )
        small_grads[layer_num] = (
            d_conv_w[:, :local_inner],
            d_conv_b[:local_inner],
            d_gate_gain,
            d_dt_bias,
            d_log_rate,
            d_skip_grad,
            d_conv_w[:, local_inner:],
            d_conv_b[local_inner:],
            d_norm_gain,
        )

    small = [jnp.stack([small_grads[l][m] for l in range(layers)]) for m in range(9)]
    flat = jnp.concatenate([s.reshape(-1) for s in small])
    flat = jnp.pad(flat, (0, -flat.shape[0] % 1024)).reshape(-1, 128)
    reduced = exchange(
        [(g, True, True) for g in weight_grads] + [(flat, False, True)], "dp", next(ids)
    )
    grads, flat = jnp.stack(reduced[:layers]), reduced[layers]
    d_bc = grads[:, :, at_bc:at_dt].astype(jnp.bfloat16)
    flats, bc_total = exchange(
        [(flat, False, False), (d_bc, False, True)], "tensor", next(ids)
    )
    flats = flats.reshape(tensor_count, -1)
    totals, start = [], 0
    for m, s in enumerate(small):
        piece = flats[:, start : start + s.size].reshape((tensor_count,) + s.shape)
        start += s.size
        if m < 6:
            joined_up = jnp.moveaxis(piece, 0, -2)
            totals.append(joined_up.reshape(s.shape[:-1] + (tensor_count * s.shape[-1],)))
        else:
            totals.append(jnp.sum(piece, axis=0))
    return (
        y_out,
        grad_hidden,
        totals[8],
        grads[:, :, :at_bc].reshape(layers, -1, 2, local_inner),
        grads[:, :, at_dt : at_dt + local_heads],
        bc_total,
        totals[0],
        totals[1],
        totals[6],
        totals[7],
        totals[3],
        totals[4],
        totals[5],
        totals[2],
        jnp.swapaxes(grads[:, :, at_out:], 1, 2),
    )


def solution(mesh):
    return jax.shard_map(
        local,
        mesh=mesh,
        in_specs=(
            P(("dp", "tensor"), None),
            P("dp"),
            P(),
            P(None, "dp", None, "tensor"),
            P(None, "dp", "tensor"),
            P(None, "dp", None),
            P(None, None, "tensor"),
            P(None, "tensor"),
            P(),
            P(),
            P(None, "tensor"),
            P(None, "tensor"),
            P(None, "tensor"),
            P(None, "tensor"),
            P(None, "tensor", "dp"),
            P(("dp", "tensor"), None),
        ),
        out_specs=(
            P(("dp", "tensor"), None),
            P(("dp", "tensor"), None),
            P(),
            P(None, "dp", None, "tensor"),
            P(None, "dp", "tensor"),
            P(None, "dp", None),
            P(),
            P(),
            P(),
            P(),
            P(),
            P(),
            P(),
            P(),
            P(None, "tensor", "dp"),
        ),
        check_vma=False,
    )
```

```python
import jax
import jax.numpy as jnp
from jax import lax
from jax.experimental import pallas as pl
from jax.experimental.pallas import tpu as pltpu
from jax.sharding import PartitionSpec as P

EPSILON = 1e-05
PRECISE = lax.Precision.HIGHEST
CORE = lax.Precision.HIGH
MESH = pl.DeviceIdType.MESH


def add_up(slots, result, count):
    rows = result.shape[0]
    tile = 32

    def some(rows_of):
        total = slots[(0, *rows_of)].astype(jnp.float32)
        for source in range(1, count):
            total = total + slots[(source, *rows_of)].astype(jnp.float32)
        result[rows_of] = total

    if result.ndim == 2 and rows % tile == 0 and rows > tile:

        @pl.loop(0, rows // tile)
        def _(index):
            some((pl.ds(pl.multiple_of(index * tile, tile), tile), slice(None)))

    else:
        some((slice(None),) * result.ndim)


def exchange(parts, collective_id):
    axes = sorted({axis for _, axis, _, _ in parts})
    counts = {axis: lax.axis_size(axis) for axis in axes}
    most = max(counts.values())
    many = len(parts)
    block_shapes = [a.shape[1:] if scatter else a.shape for a, _, scatter, _ in parts]
    outs, slots = [], []
    for (a, axis, _, reduce), shape in zip(parts, block_shapes):
        count = counts[axis]
        if reduce:
            outs.append(jax.ShapeDtypeStruct(shape, jnp.float32))
            slots.append(pltpu.VMEM((count,) + shape, a.dtype))
        else:
            outs.append(jax.ShapeDtypeStruct((count,) + shape, a.dtype))

    def kernel(*refs):
        ins, results = refs[:many], refs[many : 2 * many]
        scratch = list(refs[2 * many : len(refs) - 3])
        send_sem, recv_sem, own_sem = refs[len(refs) - 3 :]
        landing = [
            scratch.pop(0) if reduce else results[i] for i, (_, _, _, reduce) in enumerate(parts)
        ]
        places = {axis: lax.axis_index(axis) for axis in axes}
        barrier = pltpu.get_barrier_semaphore()
        for axis in axes:
            for step in range(1, counts[axis]):
                peer = lax.rem(places[axis] + step, counts[axis])
                pl.semaphore_signal(barrier, inc=1, device_id={axis: peer}, device_id_type=MESH)
        own = []
        for i, (_, axis, scatter, _) in enumerate(parts):
            me = places[axis]
            block = ins[i].at[me] if scatter else ins[i]
            copy = pltpu.make_async_copy(block, landing[i].at[me], own_sem.at[i])
            copy.start()
            own.append(copy)
        pl.semaphore_wait(barrier, sum(counts[axis] - 1 for axis in axes))
        sent = []
        for step in range(1, most):
            for i, (_, axis, scatter, _) in enumerate(parts):
                if step >= counts[axis]:
                    continue
                me = places[axis]
                peer = lax.rem(me + step, counts[axis])
                copy = pltpu.make_async_remote_copy(
                    src_ref=ins[i].at[peer] if scatter else ins[i],
                    dst_ref=landing[i].at[me],
                    send_sem=send_sem.at[i, step - 1],
                    recv_sem=recv_sem.at[i, step - 1],
                    device_id={axis: peer},
                    device_id_type=MESH,
                )
                copy.start()
                sent.append(copy)
        for copy in own:
            copy.wait()
        for copy in sent:
            copy.wait()
        for i, (_, axis, _, reduce) in enumerate(parts):
            if reduce:
                add_up(landing[i], results[i], counts[axis])

    return pl.pallas_call(
        kernel,
        out_shape=tuple(outs),
        in_specs=[pl.BlockSpec(memory_space=pltpu.VMEM)] * many,
        out_specs=tuple([pl.BlockSpec(memory_space=pltpu.VMEM)] * many),
        scratch_shapes=slots
        + [
            pltpu.SemaphoreType.DMA((many, most - 1)),
            pltpu.SemaphoreType.DMA((many, most - 1)),
            pltpu.SemaphoreType.DMA((many,)),
        ],
        compiler_params=pltpu.CompilerParams(collective_id=collective_id, has_side_effects=True),
    )(*[a for a, _, _, _ in parts])


def rows_from_all(rows, collective_id, extra=()):
    out, *others = exchange([(rows, "tensor", False, False), *extra], collective_id)
    return (out.reshape(-1, rows.shape[1]), others)


def rows_summed(partial_rows, collective_id, extra=()):
    count = lax.axis_size("tensor")
    blocks = partial_rows.astype(jnp.bfloat16).reshape(count, -1, partial_rows.shape[1])
    out, *others = exchange([(blocks, "tensor", True, True), *extra], collective_id)
    return (out, others)


def token_sums(values, collective_id, extra=()):
    out, *others = exchange([(values.reshape(-1, 128), "tensor", False, True), *extra], collective_id)
    return (out.reshape(values.shape[0]), others)


def passed_along(block, axis, distance):
    devices = range(lax.axis_size(axis))
    route = [(i - distance, i) for i in devices if i - distance in devices]
    return lax.ppermute(block, axis, route)


def entering(coefficients, values, backward):
    count = values.shape[0]
    place = lax.axis_index("dp")
    state = jnp.zeros(values.shape[1:], jnp.float32)
    for source in reversed(range(count)) if backward else range(count):
        ahead = source > place if backward else source < place
        later = values[source].astype(jnp.float32) + coefficients[source][:, None, None] * state
        state = jnp.where(ahead, later, state)
    return state


def mixer_core(xs_heads, b_mat, c_mat, step_dt, log_decay, skip_gain, segments):
    length = segments.shape[0]
    places = jnp.arange(length)
    below = places[:, None] >= places[None, :]
    cumulative = jnp.dot(below.astype(jnp.float32), log_decay, precision=PRECISE)
    inside = (segments[:, None] == segments[None, :]) & below
    by_head = cumulative.T
    span_logs = by_head[:, :, None] - by_head[:, None, :]
    decays = jnp.exp(jnp.where(inside[None], span_logs, -1e30))
    scores = jnp.dot(c_mat, b_mat.T, precision=CORE)
    scaled = xs_heads * step_dt[:, :, None]
    output = jnp.einsum("hij,jhp->ihp", decays * scores[None], scaled, precision=CORE)
    output = output + skip_gain[None, :, None] * xs_heads
    kept_rows = (segments == segments[length - 1]).astype(jnp.float32)
    to_end = jnp.exp(cumulative[length - 1][None, :] - cumulative) * kept_rows[:, None]
    state = jnp.einsum("jhp,jn->hpn", scaled * to_end[:, :, None], b_mat, precision=CORE)
    return (output, state, cumulative)


def init_output(cumulative, c_mat, start_state, segments):
    reached = (segments == segments[0]).astype(jnp.float32)
    carried = jnp.einsum("tn,hpn->thp", c_mat, start_state, precision=CORE)
    return (jnp.exp(cumulative) * reached[:, None])[:, :, None] * carried


def conv_apply(extended, seg_extended, segments, conv_weight, conv_bias):
    length = segments.shape[0]
    tap_count = conv_weight.shape[0]
    result = jnp.zeros((length, extended.shape[1]), jnp.float32) + conv_bias
    for tap_index in range(tap_count):
        same_seg = (seg_extended[tap_index : tap_index + length] == segments).astype(jnp.float32)
        result = (
            result
            + conv_weight[tap_index] * extended[tap_index : tap_index + length] * same_seg[:, None]
        )
    return result


def mixer_front(
    extended,
    proj_dt,
    conv_weight,
    conv_bias,
    bias_dt,
    log_rate,
    seg_extended,
    segments,
    head_count,
    inner_width,
):
    activated = jax.nn.silu(conv_apply(extended, seg_extended, segments, conv_weight, conv_bias))
    length = segments.shape[0]
    state_width = (activated.shape[1] - inner_width) // 2
    xs_heads = activated[:, :inner_width].reshape(length, head_count, inner_width // head_count)
    b_mat = activated[:, inner_width : inner_width + state_width]
    c_mat = activated[:, inner_width + state_width :]
    step_dt = jax.nn.softplus(proj_dt + bias_dt)
    log_decay = -step_dt * jnp.exp(log_rate)
    return (xs_heads, b_mat, c_mat, step_dt, log_decay)


def local(
    x_in,
    segment_ids,
    norm_gain,
    w_zx,
    w_dt,
    w_bc,
    conv_x,
    conv_x_bias,
    conv_bc,
    conv_bc_bias,
    dt_bias,
    a_log,
    d_skip,
    gate_gain,
    w_out,
    cotangent,
):
    layers = norm_gain.shape[0]
    tensor_count = lax.axis_size("tensor")
    data_count = lax.axis_size("dp")
    model_width = x_in.shape[1]
    shard_rows = segment_ids.shape[0]
    local_inner = conv_x.shape[2]
    local_heads = dt_bias.shape[1]
    state_pair = w_bc.shape[2]
    state_width = state_pair // 2
    head_width = local_inner // local_heads
    full_inner = local_inner * tensor_count
    margin = conv_x.shape[1] - 1
    dt_room = -local_heads % 128 + local_heads
    at_bc = 2 * local_inner
    at_dt = at_bc + state_pair
    at_out = at_dt + dt_room
    ids = iter(range(1, 64))

    packed = [
        jnp.concatenate(
            [
                w_zx[l].reshape(-1, at_bc),
                w_bc[l],
                jnp.pad(w_dt[l], ((0, 0), (0, dt_room - local_heads))),
            ],
            axis=1,
        )
        for l in range(layers)
    ]
    later_weights = [
        lax.all_gather(
            jnp.concatenate([packed[l], w_out[l].T], axis=1), "dp", axis=0, tiled=True
        )
        for l in range(1, layers)
    ]

    seg_tail = (segment_ids[shard_rows - margin :] + 1).astype(jnp.bfloat16)
    tail_segs = passed_along(seg_tail, "dp", 1)
    seg_extended = jnp.concatenate([tail_segs.astype(jnp.int32) - 1, segment_ids])
    joined = (seg_extended[margin - 1] == segment_ids[0]).astype(jnp.float32)
    whole_seg = (segment_ids[shard_rows - 1] == segment_ids[0]).astype(jnp.float32)

    hidden = x_in.astype(jnp.float32)
    records = []
    for layer_num in range(layers):
        rms_scale = lax.rsqrt(jnp.mean(hidden * hidden, axis=1, keepdims=True) + EPSILON)
        normed = (hidden * rms_scale * norm_gain[layer_num]).astype(jnp.bfloat16)
        if layer_num == 0:
            gathered, (w_in,) = rows_from_all(
                normed, next(ids), [(packed[0], "dp", False, False)]
            )
            w_in = w_in.reshape(model_width, at_out)
            ride = [(w_out[0].T, "dp", False, False)]
        else:
            gathered, _ = rows_from_all(normed, next(ids))
            full = later_weights[layer_num - 1]
            w_in, w_back = full[:, :at_out], full[:, at_out:]
            ride = []
        projected = jnp.dot(gathered, w_in, preferred_element_type=jnp.float32)
        proj_z = projected[:, :local_inner]
        proj_dt = projected[:, at_dt : at_dt + local_heads]
        conv_in = projected[:, local_inner:at_dt].astype(jnp.bfloat16)
        tail_rows = passed_along(conv_in[shard_rows - margin :], "dp", 1)
        extended = jnp.concatenate([tail_rows, conv_in], axis=0).astype(jnp.float32)
        conv_weight = jnp.concatenate([conv_x[layer_num], conv_bc[layer_num]], axis=1)
        conv_bias = jnp.concatenate([conv_x_bias[layer_num], conv_bc_bias[layer_num]])

        def front_fn(extended, proj_dt, conv_weight, conv_bias, bias_dt, log_rate):
            return mixer_front(
                extended,
                proj_dt,
                conv_weight,
                conv_bias,
                bias_dt,
                log_rate,
                seg_extended,
                segment_ids,
                local_heads,
                local_inner,
            )

        front_vals, front_back = jax.vjp(
            front_fn,
            extended,
            proj_dt,
            conv_weight,
            conv_bias,
            dt_bias[layer_num],
            a_log[layer_num],
        )
        xs_heads, b_mat, c_mat, step_dt, log_decay = front_vals
        core_vals, core_back = jax.vjp(
            lambda *args: mixer_core(*args, segment_ids),
            xs_heads,
            b_mat,
            c_mat,
            step_dt,
            log_decay,
            d_skip[layer_num],
        )
        local_y, local_state, cumulative = core_vals
        end_decay = jnp.exp(cumulative[shard_rows - 1])
        coefficient = joined * whole_seg * end_decay
        pieces = [
            (
                jnp.pad(coefficient, (0, dt_room - local_heads)).reshape(-1, 128),
                "dp",
                False,
                False,
            ),
            (
                local_state.astype(jnp.bfloat16).reshape(local_inner, state_width),
                "dp",
                False,
                False,
            ),
        ]
        if layer_num == 0:
            pieces.append((cotangent, "tensor", False, False))
        coefficients, states, *others = exchange(pieces, next(ids))
        if layer_num == 0:
            last_branch_grad = others[0].reshape(-1, model_width)
        coefficients = coefficients.reshape(data_count, dt_room)[:, :local_heads]
        states = states.reshape(data_count, local_heads, head_width, state_width)
        start_state = joined * entering(coefficients, states, False)
        init_y, init_back = jax.vjp(
            lambda *args: init_output(*args, segment_ids), cumulative, c_mat, start_state
        )
        ssd_y = (local_y + init_y).reshape(shard_rows, local_inner)
        gate_vals = jax.nn.silu(proj_z)
        gated_y = ssd_y * gate_vals
        squares, others = token_sums(jnp.sum(gated_y * gated_y, axis=1), next(ids), ride)
        if layer_num == 0:
            w_back = others[0].reshape(model_width, local_inner)
        inverse = lax.rsqrt(squares / full_inner + EPSILON)
        mixed_out = (gated_y * inverse[:, None] * gate_gain[layer_num]).astype(jnp.bfloat16)
        branch, _ = rows_summed(
            jnp.einsum(
                "tk,dk->td",
                mixed_out,
                w_back,
                preferred_element_type=jnp.float32,
            ),
            next(ids),
        )
        records.append(
            (
                w_in,
                w_back,
                hidden,
                gathered,
                proj_z,
                ssd_y,
                gate_vals,
                gated_y,
                mixed_out,
                inverse,
                start_state,
                end_decay,
                coefficients,
                front_back,
                core_back,
                init_back,
            )
        )
        hidden = hidden + branch
    y_out = hidden.astype(jnp.bfloat16)
    grad_hidden = cotangent.astype(jnp.float32)

    def by_owner(grad):
        blocks = grad.astype(jnp.bfloat16).reshape(data_count, -1, grad.shape[1])
        return (blocks, "dp", True, True)

    small_grads = [None] * layers
    waiting = []
    summed = {}
    for layer_num in reversed(range(layers)):
        (
            w_in,
            w_back,
            hidden_in,
            gathered,
            proj_z,
            ssd_y,
            gate_vals,
            gated_y,
            mixed_out,
            inverse,
            start_state,
            end_decay,
            coefficients,
            front_back,
            core_back,
            init_back,
        ) = records[layer_num]
        riders = waiting[:2]
        if layer_num == layers - 1:
            branch_grad = last_branch_grad
        else:
            branch_grad, others = rows_from_all(
                grad_hidden.astype(jnp.bfloat16), next(ids), [r[1] for r in riders]
            )
            summed.update(zip([r[0] for r in riders], others))
        waiting = waiting[2:]
        d_out = jnp.einsum("td,tk->dk", branch_grad, mixed_out, preferred_element_type=jnp.float32)
        d_mixed = jnp.einsum(
            "td,dk->tk", branch_grad, w_back, preferred_element_type=jnp.float32
        )
        weighted = d_mixed * gate_gain[layer_num]
        riders, waiting = waiting[:1], waiting[1:]
        inner_dot, others = token_sums(
            jnp.sum(weighted * gated_y, axis=1), next(ids), [r[1] for r in riders]
        )
        summed.update(zip([r[0] for r in riders], others))
        d_gated = (
            inverse[:, None] * weighted
            - gated_y * (inverse * inverse * inverse * inner_dot / full_inner)[:, None]
        )
        d_gate_gain = jnp.sum(d_mixed * gated_y * inverse[:, None], axis=0)
        d_ssd = d_gated * gate_vals
        sigmoid_z = jax.nn.sigmoid(proj_z)
        d_proj_z = (d_gated * ssd_y * sigmoid_z * (1.0 + proj_z * (1.0 - sigmoid_z))).astype(
            jnp.bfloat16
        )
        d_heads = d_ssd.reshape(shard_rows, local_heads, head_width)
        d_cum, d_cmat_first, d_start = init_back(d_heads)
        (d_states,) = exchange(
            [
                (
                    (joined * d_start).astype(jnp.bfloat16).reshape(local_inner, state_width),
                    "dp",
                    False,
                    False,
                )
            ],
            next(ids),
        )
        d_end = entering(
            coefficients,
            d_states.reshape(data_count, local_heads, head_width, state_width),
            True,
        )
        d_last = whole_seg * end_decay * jnp.sum(d_end * start_state, axis=(1, 2))
        d_cum = d_cum + jnp.where(
            jnp.arange(shard_rows)[:, None] == shard_rows - 1, d_last[None, :], 0.0
        )
        d_xs, d_bmat, d_cmat_second, d_dt, d_decay, d_skip_grad = core_back((d_heads, d_end, d_cum))
        d_ext, d_proj_dt, d_conv_w, d_conv_b, d_dt_bias, d_log_rate = front_back(
            (d_xs, d_bmat, d_cmat_first + d_cmat_second, d_dt, d_decay)
        )
        from_next = passed_along(d_ext[:margin], "dp", -1)
        d_conv_in = d_ext[margin:]
        d_conv_in = jnp.concatenate(
            [d_conv_in[: shard_rows - margin], d_conv_in[shard_rows - margin :] + from_next], axis=0
        )
        d_proj_bc = d_conv_in[:, local_inner:]
        bc_high = d_proj_bc.astype(jnp.bfloat16)
        bc_rest = (d_proj_bc - bc_high.astype(jnp.float32)).astype(jnp.bfloat16)
        d_all = jnp.concatenate(
            [
                d_proj_z,
                d_conv_in[:, :local_inner].astype(jnp.bfloat16),
                bc_high,
                jnp.pad(
                    d_proj_dt.astype(jnp.bfloat16), ((0, 0), (0, dt_room - local_heads))
                ),
            ],
            axis=1,
        )
        waiting.append(((layer_num, 3), by_owner(d_out)))
        riders, waiting = waiting[:2], waiting[2:]
        d_normed, others = rows_summed(
            jnp.einsum(
                "tk,dk->td", d_all, w_in, preferred_element_type=jnp.float32
            )
            + jnp.einsum(
                "tk,dk->td", bc_rest, w_in[:, at_bc:at_dt], preferred_element_type=jnp.float32
            ),
            next(ids),
            [r[1] for r in riders],
        )
        summed.update(zip([r[0] for r in riders], others))
        d_in = jnp.einsum("td,tk->dk", gathered, d_all, preferred_element_type=jnp.float32)
        d_rest = jnp.einsum("td,tk->dk", gathered, bc_rest, preferred_element_type=jnp.float32)
        d_maps = jnp.concatenate([d_in[:, at_bc:at_dt] + d_rest, d_in[:, at_dt:]], axis=1)
        waiting += [
            ((layer_num, 0), by_owner(d_in[:, :local_inner])),
            ((layer_num, 1), by_owner(d_in[:, local_inner:at_bc])),
            ((layer_num, 2), by_owner(d_maps)),
        ]
        rms_scale = lax.rsqrt(jnp.mean(hidden_in * hidden_in, axis=1, keepdims=True) + EPSILON)
        gain_grad_in = d_normed * norm_gain[layer_num]
        d_norm_gain = jnp.sum(d_normed * hidden_in * rms_scale, axis=0)
        grad_hidden = (
            grad_hidden
            + rms_scale * gain_grad_in
            - hidden_in
            * rms_scale
            * rms_scale
            * rms_scale
            * jnp.mean(gain_grad_in * hidden_in, axis=1, keepdims=True)
        )
        small_grads[layer_num] = (
            d_conv_w[:, :local_inner],
            d_conv_b[:local_inner],
            d_gate_gain,
            d_dt_bias,
            d_log_rate,
            d_skip_grad,
            d_conv_w[:, local_inner:],
            d_conv_b[local_inner:],
            d_norm_gain,
        )

    small = [jnp.stack([small_grads[l][m] for l in range(layers)]) for m in range(9)]
    flat = jnp.concatenate([s.reshape(-1) for s in small])
    flat = jnp.pad(flat, (0, -flat.shape[0] % 1024)).reshape(-1, 128)
    flat, *others = exchange(
        [(flat, "dp", False, True)] + [r[1] for r in waiting], next(ids)
    )
    summed.update(zip([r[0] for r in waiting], others))
    grads = [jnp.stack([summed[(l, m)] for l in range(layers)]) for m in range(4)]
    d_bc = grads[2][:, :, :state_pair].astype(jnp.bfloat16)
    flats, bc_total = exchange(
        [(flat, "tensor", False, False), (d_bc, "tensor", False, True)], next(ids)
    )
    flats = flats.reshape(tensor_count, -1)
    totals, start = [], 0
    for m, s in enumerate(small):
        piece = flats[:, start : start + s.size].reshape((tensor_count,) + s.shape)
        start += s.size
        if m < 6:
            joined_up = jnp.moveaxis(piece, 0, -2)
            totals.append(joined_up.reshape(s.shape[:-1] + (tensor_count * s.shape[-1],)))
        else:
            totals.append(jnp.sum(piece, axis=0))
    return (
        y_out,
        grad_hidden,
        totals[8],
        jnp.stack([grads[0], grads[1]], axis=2),
        grads[2][:, :, state_pair : state_pair + local_heads],
        bc_total,
        totals[0],
        totals[1],
        totals[6],
        totals[7],
        totals[3],
        totals[4],
        totals[5],
        totals[2],
        jnp.swapaxes(grads[3], 1, 2),
    )


def solution(mesh):
    return jax.shard_map(
        local,
        mesh=mesh,
        in_specs=(
            P(("dp", "tensor"), None),
            P("dp"),
            P(),
            P(None, "dp", None, "tensor"),
            P(None, "dp", "tensor"),
            P(None, "dp", None),
            P(None, None, "tensor"),
            P(None, "tensor"),
            P(),
            P(),
            P(None, "tensor"),
            P(None, "tensor"),
            P(None, "tensor"),
            P(None, "tensor"),
            P(None, "tensor", "dp"),
            P(("dp", "tensor"), None),
        ),
        out_specs=(
            P(("dp", "tensor"), None),
            P(("dp", "tensor"), None),
            P(),
            P(None, "dp", None, "tensor"),
            P(None, "dp", "tensor"),
            P(None, "dp", None),
            P(),
            P(),
            P(),
            P(),
            P(),
            P(),
            P(),
            P(),
            P(None, "tensor", "dp"),
        ),
        check_vma=False,
    )
```
